512 devices in a mesh: dp: 32 (over z, x_hi), tensor: 16 (over x_lo, y, core).
Axes of the slice: x: 4 (x_hi: 2, x_lo: 2; x = x_hi * 2 + x_lo), y: 4, z: 16, core: 2. Of those that a mesh axis runs over, the one named last changes fastest.
Arguments:
- activations: bfloat16 [2, 128, 256, 4096], P(None, 'dp', None, 'tensor'), may hold values from -6 to 6
- out_grads: bfloat16 [2, 128, 256, 4096], P(None, 'dp', None, 'tensor'), may hold values from -6 to 6
- proj_in: bfloat16 [2, 4096, 64], P(None, 'tensor'), may hold values from -0.09375 to 0.09375
- proj_out: bfloat16 [2, 4096, 64], P(None, 'tensor'), may hold values from -0.09375 to 0.09375
- lengths: int32 [128], P('dp'), may hold values from 32 to 256, as said below
- test_feats: bfloat16 [2, 8192, 4096], P(None, 'dp'), may hold values from -0.0059814453 to 0.0059814453
- test_slot: int32 [8192], P('dp'), may hold values from 0 to 255, as said below
Outputs:
- scores: float32 [128, 1024], P('dp')
The draws below stay inside these ranges and needn't reach their ends.
Inputs may be any that keep to these rules, and one draw needn't show every extreme that they name: Positions from lengths[e] on are padding; some example has exactly 256 real tokens and some exactly 32. `test_slot`: within each aligned block of 256 test items a permutation of 0 to 255.
All inputs are finite; a program needn't handle non-finite values.
Results may differ from the reference program's by a relative error of at most 0.005.
Values may be sent and summed in bfloat16 or wider, within the bound.
No kernel may reach another device: no remote copies, remote signals or barrier semaphores. Data moves between devices by JAX's collectives and lax.ppermute only.
A program may use at most 128 MiB of HBM per device.

```python
import jax
import jax.numpy as jnp
from jax import lax

D = 4096
RANK = 64
LAYERS = 2
STEPS = 4
EX_DEV = 4
SEQ = 256
TB = 256
FEAT = 4096
TRAIN = 128
TEST = 8192
N_DP = 32


def draw_lengths(key, part):
    first_key, second_key, third_key = jax.random.split(key, 3)
    drawn = jax.random.randint(first_key, (TRAIN,), SEQ // 8, SEQ + 1)
    longest = jax.random.randint(second_key, (), 0, TRAIN)
    shortest = (longest + 1 + jax.random.randint(third_key, (), 0, TRAIN - 1)) % TRAIN
    position = jnp.arange(TRAIN)
    drawn = jnp.where(position == longest, SEQ, drawn)
    drawn = jnp.where(position == shortest, SEQ // 8, drawn)
    return drawn.astype(jnp.int32)


def draw_test_slot(key, part):
    block_keys = jax.random.split(key, TEST // TB)
    orders = jax.vmap(lambda one_key: jax.random.permutation(one_key, TB))(block_keys)
    return orders.reshape(TEST).astype(jnp.int32)


def levels(rng, extent, cuts, least, largest):
    def one(dim, blocks):
        heights = jax.random.uniform(jax.random.fold_in(jax.random.fold_in(rng, 6), dim), (blocks,), jnp.float32, least / len(cuts), largest / len(cuts))
        return jnp.repeat(jnp.exp(heights), extent[dim] // blocks).reshape((-1,) + (1,) * (len(extent) - dim - 1))

    gain = one(*cuts[0])
    for cut in cuts[1:]:
        gain = gain * one(*cut)
    return gain


def scatter_about(key, extent, scale, bound, cuts=(), kind=jnp.bfloat16):
    factor_of = levels(key, extent, cuts, -0.22, 0.18) if cuts else 1.0
    values = jax.random.normal(key, extent, jnp.float32) * scale * factor_of
    return jnp.minimum(jnp.maximum(values, -bound), bound).astype(kind)


def setup_inputs(seed: int = 0) -> dict:
    seeds = jax.random.split(jax.random.key(seed), 8)
    return {
        "activations": scatter_about(seeds[0], (LAYERS, TRAIN, SEQ, D), 1.0, 6.0, ((1, 32), (3, 16))),
        "out_grads": scatter_about(seeds[1], (LAYERS, TRAIN, SEQ, D), 1.0, 6.0, ((1, 32), (3, 16))),
        "proj_in": scatter_about(seeds[2], (LAYERS, D, RANK), D ** -0.5, 0.09375, ((1, 16),)),
        "proj_out": scatter_about(seeds[3], (LAYERS, D, RANK), D ** -0.5, 0.09375, ((1, 16),)),
        "lengths": draw_lengths(jax.random.fold_in(seeds[7], 71), 0),
        "test_feats": scatter_about(seeds[5], (LAYERS, TEST, FEAT), 0.001, 0.0059814453, ((1, 32),)),
        "test_slot": draw_test_slot(jax.random.fold_in(seeds[7], 71), 0),
    }


def project(values, matrix):
    flat = jnp.dot(values.reshape(-1, D), matrix, preferred_element_type=jnp.float32)
    rounded = lax.optimization_barrier(flat.astype(jnp.bfloat16))
    return rounded.astype(jnp.float32).reshape(TRAIN, SEQ, RANK)


def reference(activations, out_grads, proj_in, proj_out, lengths, test_feats, test_slot):
    positions = jnp.arange(SEQ, dtype=jnp.int32)
    kept_mask = (positions[None, :] < lengths[:, None]).astype(jnp.float32)
    layer_feats = []
    for layer_index in range(LAYERS):
        act_proj = project(activations[layer_index], proj_in[layer_index])
        grad_proj = project(out_grads[layer_index], proj_out[layer_index]) * kept_mask[:, :, None]
        outer_sums = jnp.einsum("esa,esb->eab", grad_proj, act_proj, precision=lax.Precision.HIGHEST)
        layer_feats.append(outer_sums.reshape(TRAIN, FEAT).astype(jnp.bfloat16))
    features = jnp.concatenate(layer_feats, axis=1)
    test_flat = jnp.transpose(test_feats, (1, 0, 2)).reshape(TEST, LAYERS * FEAT)
    target = (jnp.arange(TEST, dtype=jnp.int32) // TB) * TB + test_slot
    ordered = jnp.zeros_like(test_flat).at[target].set(test_flat)
    all_scores = jnp.dot(features, ordered.T, preferred_element_type=jnp.float32)
    shard_of = jnp.arange(TRAIN, dtype=jnp.int32) // EX_DEV
    tile_index = jnp.arange(STEPS, dtype=jnp.int32)
    source = (shard_of[:, None] - tile_index[None, :]) % N_DP
    columns = source[:, :, None] * TB + jnp.arange(TB, dtype=jnp.int32)[None, None, :]
    columns = columns.reshape(TRAIN, STEPS * TB).astype(jnp.int32)
    return jnp.take_along_axis(all_scores, columns, axis=1)
```

```python
import jax
import jax.numpy as jnp
from jax import lax
from jax.sharding import PartitionSpec as P

STEPS = 4
GROUP = 16
HIGH = lax.Precision.HIGHEST


def role(k):
    y0, core = (k >> 1) & 1, k & 1
    tile = y0 + core * (3 - 2 * y0)
    return tile, (k >> 2) & 1


def block_pairs(dp_size):
    pairs = []
    for shard in range(dp_size):
        for k in range(GROUP):
            tile, _ = role(k)
            source = k ^ (8 * (tile & 1))
            pairs.append((((shard - tile) % dp_size) * GROUP + source, shard * GROUP + k))
    return pairs


def split_dot(rows, block):
    high = rows.astype(jnp.bfloat16)
    low = (rows - high.astype(jnp.float32)).astype(jnp.bfloat16)
    both = jnp.concatenate([high, low], axis=0)
    out = jnp.einsum("ef,tf->et", both, block, preferred_element_type=jnp.float32)
    return out[: rows.shape[0]] + out[rows.shape[0] :]


def shards(activations, out_grads, proj_in, proj_out, lengths, test_feats, test_slot):
    layers, examples, tokens, _ = activations.shape
    rank = proj_in.shape[2]
    block, feats = test_feats.shape[1], test_feats.shape[2]
    half_feats, half_tokens = feats // 2, tokens // 2
    k = lax.axis_index("tensor")

    tile, half = role(k)
    layer = (k >> 3) ^ (tile & 1)
    piece = lax.dynamic_slice(test_feats, (layer, 0, half * half_feats), (1, block, half_feats))[0]
    place = (jnp.arange(block, dtype=jnp.int32)[:, None] == test_slot[None, :]).astype(jnp.bfloat16)
    ordered = jnp.dot(place, piece, preferred_element_type=jnp.float32).astype(jnp.bfloat16)
    test_block = lax.ppermute(ordered, ("dp", "tensor"), block_pairs(lax.axis_size("dp")))

    part_act = jnp.einsum("lesd,ldr->lesr", activations, proj_in, preferred_element_type=jnp.float32)
    part_grad = jnp.einsum("lesd,ldr->lesr", out_grads, proj_out, preferred_element_type=jnp.float32)
    part = jnp.concatenate([part_act, part_grad], axis=3).astype(jnp.bfloat16)
    part = part.reshape(GROUP, half_tokens, 2 * rank)
    part = lax.all_to_all(part, "tensor", 0, 0)
    proj = jnp.sum(part.astype(jnp.float32), axis=0)
    position = (k & 1) * half_tokens + jnp.arange(half_tokens, dtype=jnp.int32)
    kept = position < lengths[(k >> 1) & 3]
    grad = jnp.where(kept[:, None], proj[:, rank:], 0.0)
    outer = jnp.einsum("sa,sb->ab", grad, proj[:, :rank], precision=HIGH)
    outer = outer.reshape(2, 1, rank // 4, 2 * rank)
    outer = jnp.broadcast_to(outer, (2, 4, rank // 4, 2 * rank)).reshape(8, rank // 4, 2 * rank)
    groups = [list(range(8)), list(range(8, 16))]
    outer = lax.all_to_all(outer, "tensor", 0, 0, axis_index_groups=groups)
    features = outer.reshape(examples, 2, half_feats).sum(axis=1)

    scores = split_dot(features, test_block)
    scores = lax.all_to_all(jnp.broadcast_to(scores[None], (GROUP, examples, block)), "tensor", 0, 0)
    scores = scores.reshape(2, 2, 4, examples, block).sum(axis=(0, 1))
    return jnp.concatenate([scores[0], scores[2], scores[3], scores[1]], axis=1)


def solution(mesh):
    return jax.shard_map(
        shards,
        mesh=mesh,
        in_specs=(
            P(None, "dp", None, "tensor"),
            P(None, "dp", None, "tensor"),
            P(None, "tensor", None),
            P(None, "tensor", None),
            P("dp"),
            P(None, "dp", None),
            P("dp"),
        ),
        out_specs=P("dp", None),
        check_vma=False,
    )
```

```python
import jax
import jax.numpy as jnp
from jax import lax
from jax.experimental import pallas as pl
from jax.experimental.pallas import tpu as pltpu
from jax.sharding import PartitionSpec as P

GROUP = 16
HIGH = lax.Precision.HIGHEST


def role(k):
    y0, core = (k >> 1) & 1, k & 1
    tile = y0 + core * (3 - 2 * y0)
    return tile, (k >> 2) & 1


def block_pairs(dp_size):
    pairs = []
    for shard in range(dp_size):
        for k in range(GROUP):
            tile, _ = role(k)
            source = k ^ (8 * (tile & 1))
            pairs.append((((shard - tile) % dp_size) * GROUP + source, shard * GROUP + k))
    return pairs


def split_dot(rows, block):
    high = rows.astype(jnp.bfloat16)
    low = (rows - high.astype(jnp.float32)).astype(jnp.bfloat16)
    both = jnp.concatenate([high, low], axis=0)
    out = jnp.einsum("ef,tf->et", both, block, preferred_element_type=jnp.float32)
    return out[: rows.shape[0]] + out[rows.shape[0] :]


def project_kernel(act_hbm, grad_hbm, in_hbm, out_hbm, part_ref, rows, matrices, sems):
    layers, examples, tokens, width = act_hbm.shape
    rank = in_hbm.shape[1]
    count = layers * examples
    loads = [
        pltpu.make_async_copy(in_hbm, matrices.at[0], sems.at[2 * count]),
        pltpu.make_async_copy(out_hbm, matrices.at[1], sems.at[2 * count + 1]),
    ]
    for i in range(count):
        layer, example = divmod(i, examples)
        loads.append(pltpu.make_async_copy(act_hbm.at[layer, example], rows.at[0, i], sems.at[i]))
        loads.append(pltpu.make_async_copy(grad_hbm.at[layer, example], rows.at[1, i], sems.at[count + i]))
    for load in loads:
        load.start()
    loads[0].wait()
    loads[1].wait()
    empty = jnp.zeros((rank, width), jnp.bfloat16)
    for layer in range(layers):
        left = jnp.concatenate([matrices[0, layer], empty], axis=1)
        right = jnp.concatenate([empty, matrices[1, layer]], axis=1)
        matrix = jnp.concatenate([left, right], axis=0)
        for example in range(examples):
            i = layer * examples + example
            loads[2 * i + 2].wait()
            loads[2 * i + 3].wait()
            both = jnp.concatenate([rows[0, i], rows[1, i]], axis=1)
            part = lax.dot_general(
                both, matrix, (((1,), (1,)), ((), ())), preferred_element_type=jnp.float32
            ).astype(jnp.bfloat16)
            part_ref[2 * i] = part[: tokens // 2]
            part_ref[2 * i + 1] = part[tokens // 2 :]


def project(activations, out_grads, proj_in, proj_out):
    layers, examples, tokens, width = activations.shape
    rank = proj_in.shape[2]
    count = layers * examples
    return pl.pallas_call(
        project_kernel,
        out_shape=jax.ShapeDtypeStruct((2 * count, tokens // 2, 2 * rank), jnp.bfloat16),
        in_specs=[pl.BlockSpec(memory_space=pltpu.HBM)] * 4,
        out_specs=pl.BlockSpec(memory_space=pltpu.VMEM),
        scratch_shapes=[
            pltpu.VMEM((2, count, tokens, width), jnp.bfloat16),
            pltpu.VMEM((2, layers, rank, width), jnp.bfloat16),
            pltpu.SemaphoreType.DMA((2 * count + 2,)),
        ],
        cost_estimate=pl.CostEstimate(flops=2**29, bytes_accessed=2**21, transcendentals=0),
        name="project",
    )(activations, out_grads, jnp.swapaxes(proj_in, 1, 2), jnp.swapaxes(proj_out, 1, 2))


def shards(activations, out_grads, proj_in, proj_out, lengths, test_feats, test_slot):
    _, examples, tokens, _ = activations.shape
    rank = proj_in.shape[2]
    block, feats = test_feats.shape[1], test_feats.shape[2]
    half_feats, half_tokens = feats // 2, tokens // 2
    k = lax.axis_index("tensor")

    tile, half = role(k)
    layer = (k >> 3) ^ (tile & 1)
    piece = lax.dynamic_slice(test_feats, (layer, 0, half * half_feats), (1, block, half_feats))[0]
    place = (jnp.arange(block, dtype=jnp.int32)[:, None] == test_slot[None, :]).astype(jnp.bfloat16)
    ordered = jnp.dot(place, piece, preferred_element_type=jnp.float32).astype(jnp.bfloat16)
    test_block = lax.ppermute(ordered, ("dp", "tensor"), block_pairs(lax.axis_size("dp")))

    part = project(activations, out_grads, proj_in, proj_out)
    part = lax.all_to_all(part, "tensor", 0, 0)
    proj = jnp.sum(part.astype(jnp.float32), axis=0)
    position = (k & 1) * half_tokens + jnp.arange(half_tokens, dtype=jnp.int32)
    kept = position < lengths[(k >> 1) & 3]
    grad = jnp.where(kept[:, None], proj[:, rank:], 0.0)
    outer = jnp.einsum("sa,sb->ab", grad, proj[:, :rank], precision=HIGH)
    outer = outer.reshape(2, 1, rank // 4, 2 * rank)
    outer = jnp.broadcast_to(outer, (2, 4, rank // 4, 2 * rank)).reshape(8, rank // 4, 2 * rank)
    groups = [list(range(8)), list(range(8, 16))]
    outer = lax.all_to_all(outer, "tensor", 0, 0, axis_index_groups=groups)
    features = outer.reshape(examples, 2, half_feats).sum(axis=1)

    scores = split_dot(features, test_block)
    scores = lax.all_to_all(jnp.broadcast_to(scores[None], (GROUP, examples, block)), "tensor", 0, 0)
    scores = scores.reshape(2, 2, 4, examples, block).sum(axis=(0, 1))
    return jnp.concatenate([scores[0], scores[2], scores[3], scores[1]], axis=1)


def solution(mesh):
    return jax.shard_map(
        shards,
        mesh=mesh,
        in_specs=(
            P(None, "dp", None, "tensor"),
            P(None, "dp", None, "tensor"),
            P(None, "tensor", None),
            P(None, "tensor", None),
            P("dp"),
            P(None, "dp", None),
            P("dp"),
        ),
        out_specs=P("dp", None),
        check_vma=False,
    )
```

```python
import jax
import jax.numpy as jnp
from jax import lax
from jax.experimental import pallas as pl
from jax.experimental.pallas import tpu as pltpu
from jax.sharding import PartitionSpec as P

GROUP = 16
HIGH = lax.Precision.HIGHEST


def role(k):
    y0, core = (k >> 1) & 1, k & 1
    tile = y0 + core * (3 - 2 * y0)
    return tile, (k >> 2) & 1


def block_pairs(dp_size):
    pairs = []
    for shard in range(dp_size):
        for k in range(GROUP):
            tile, _ = role(k)
            source = k ^ (8 * (tile & 1))
            pairs.append((((shard - tile) % dp_size) * GROUP + source, shard * GROUP + k))
    return pairs


def split_dot(rows, block):
    high = rows.astype(jnp.bfloat16)
    low = (rows - high.astype(jnp.float32)).astype(jnp.bfloat16)
    both = jnp.concatenate([high, low], axis=0)
    out = jnp.einsum("ef,tf->et", both, block, preferred_element_type=jnp.float32)
    return out[: rows.shape[0]] + out[rows.shape[0] :]


def project_kernel(act_hbm, grad_hbm, in_hbm, out_hbm, part_ref, rows, matrices, sems):
    layers, examples, tokens, _ = act_hbm.shape
    rank = in_hbm.shape[1]
    count = layers * examples
    loads = [
        pltpu.make_async_copy(in_hbm, matrices.at[0], sems.at[2 * count]),
        pltpu.make_async_copy(out_hbm, matrices.at[1], sems.at[2 * count + 1]),
    ]
    for i in range(count):
        layer, example = divmod(i, examples)
        loads.append(pltpu.make_async_copy(act_hbm.at[layer, example], rows.at[0, i], sems.at[i]))
        loads.append(pltpu.make_async_copy(grad_hbm.at[layer, example], rows.at[1, i], sems.at[count + i]))
    for load in loads:
        load.start()
    loads[0].wait()
    loads[1].wait()
    for i in range(count):
        for side in range(2):
            loads[2 * i + 2 + side].wait()
            part = lax.dot_general(
                matrices[side, i // examples],
                rows[side, i],
                (((1,), (1,)), ((), ())),
                preferred_element_type=jnp.float32,
            ).astype(jnp.bfloat16)
            ranks = pl.ds(side * rank, rank)
            part_ref[2 * i, ranks] = part[:, : tokens // 2]
            part_ref[2 * i + 1, ranks] = part[:, tokens // 2 :]


def project(activations, out_grads, proj_in, proj_out):
    layers, examples, tokens, width = activations.shape
    rank = proj_in.shape[2]
    count = layers * examples
    return pl.pallas_call(
        project_kernel,
        out_shape=jax.ShapeDtypeStruct((2 * count, 2 * rank, tokens // 2), jnp.bfloat16),
        in_specs=[pl.BlockSpec(memory_space=pltpu.HBM)] * 4,
        out_specs=pl.BlockSpec(memory_space=pltpu.VMEM),
        scratch_shapes=[
            pltpu.VMEM((2, count, tokens, width), jnp.bfloat16),
            pltpu.VMEM((2, layers, rank, width), jnp.bfloat16),
            pltpu.SemaphoreType.DMA((2 * count + 2,)),
        ],
        cost_estimate=pl.CostEstimate(flops=2**29, bytes_accessed=2**21, transcendentals=0),
        name="project",
    )(activations, out_grads, jnp.swapaxes(proj_in, 1, 2), jnp.swapaxes(proj_out, 1, 2))


def shards(activations, out_grads, proj_in, proj_out, lengths, test_feats, test_slot):
    _, examples, tokens, _ = activations.shape
    rank = proj_in.shape[2]
    block, feats = test_feats.shape[1], test_feats.shape[2]
    half_feats, half_tokens = feats // 2, tokens // 2
    k = lax.axis_index("tensor")

    tile, half = role(k)
    layer = (k >> 3) ^ (tile & 1)
    piece = lax.dynamic_slice(test_feats, (layer, 0, half * half_feats), (1, block, half_feats))[0]
    place = (jnp.arange(block, dtype=jnp.int32)[:, None] == test_slot[None, :]).astype(jnp.bfloat16)
    ordered = jnp.dot(place, piece, preferred_element_type=jnp.float32).astype(jnp.bfloat16)
    test_block = lax.ppermute(ordered, ("dp", "tensor"), block_pairs(lax.axis_size("dp")))

    part = project(activations, out_grads, proj_in, proj_out)
    part = lax.all_to_all(part, "tensor", 0, 0)
    proj = jnp.sum(part.astype(jnp.float32), axis=0)
    position = (k & 1) * half_tokens + jnp.arange(half_tokens, dtype=jnp.int32)
    kept = position < lengths[(k >> 1) & 3]
    grad = jnp.where(kept[None, :], proj[rank:], 0.0)
    outer = jnp.einsum("as,bs->ab", grad, proj[:rank], precision=HIGH)
    outer = outer.reshape(2, 1, rank // 4, 2 * rank)
    outer = jnp.broadcast_to(outer, (2, 4, rank // 4, 2 * rank)).reshape(8, rank // 4, 2 * rank)
    groups = [list(range(8)), list(range(8, 16))]
    outer = lax.all_to_all(outer, "tensor", 0, 0, axis_index_groups=groups)
    features = outer.reshape(examples, 2, half_feats).sum(axis=1)

    scores = split_dot(features, test_block)
    scores = lax.all_to_all(jnp.broadcast_to(scores[None], (GROUP, examples, block)), "tensor", 0, 0)
    scores = scores.reshape(2, 2, 4, examples, block).sum(axis=(0, 1))
    return jnp.concatenate([scores[0], scores[2], scores[3], scores[1]], axis=1)


def solution(mesh):
    return jax.shard_map(
        shards,
        mesh=mesh,
        in_specs=(
            P(None, "dp", None, "tensor"),
            P(None, "dp", None, "tensor"),
            P(None, "tensor", None),
            P(None, "tensor", None),
            P("dp"),
            P(None, "dp", None),
            P("dp"),
        ),
        out_specs=P("dp", None),
        check_vma=False,
    )
```

```python
import jax
import jax.numpy as jnp
from jax import lax
from jax.sharding import PartitionSpec as P

GROUP = 16
HIGH = lax.Precision.HIGHEST


def role(k):
    y0, core = (k >> 1) & 1, k & 1
    tile = y0 + core * (3 - 2 * y0)
    return tile, (k >> 2) & 1


def block_pairs(dp_size):
    pairs = []
    for shard in range(dp_size):
        for k in range(GROUP):
            tile, _ = role(k)
            source = k ^ (8 * (tile & 1))
            pairs.append((((shard - tile) % dp_size) * GROUP + source, shard * GROUP + k))
    return pairs


def split_dot(rows, block):
    high = rows.astype(jnp.bfloat16)
    low = (rows - high.astype(jnp.float32)).astype(jnp.bfloat16)
    both = jnp.concatenate([high, low], axis=0)
    out = jnp.einsum("ef,tf->et", both, block, preferred_element_type=jnp.float32)
    return out[: rows.shape[0]] + out[rows.shape[0] :]


def project(values, matrix):
    layers, examples, tokens, width = values.shape
    halves = values.reshape(layers, examples, 2, tokens // 2, width)
    part = jnp.einsum("lehsd,ldr->lehrs", halves, matrix, preferred_element_type=jnp.float32)
    return part.astype(jnp.bfloat16)


def shards(activations, out_grads, proj_in, proj_out, lengths, test_feats, test_slot):
    _, examples, tokens, _ = activations.shape
    rank = proj_in.shape[2]
    block, feats = test_feats.shape[1], test_feats.shape[2]
    half_feats, half_tokens = feats // 2, tokens // 2
    k = lax.axis_index("tensor")

    tile, half = role(k)
    layer = (k >> 3) ^ (tile & 1)
    piece = lax.dynamic_slice(test_feats, (layer, 0, half * half_feats), (1, block, half_feats))[0]
    place = (jnp.arange(block, dtype=jnp.int32)[:, None] == test_slot[None, :]).astype(jnp.bfloat16)
    ordered = jnp.dot(place, piece, preferred_element_type=jnp.float32).astype(jnp.bfloat16)
    test_block = lax.ppermute(ordered, ("dp", "tensor"), block_pairs(lax.axis_size("dp")))

    sides = [project(activations, proj_in), project(out_grads, proj_out)]
    part = jnp.concatenate(sides, axis=3).reshape(GROUP, 2 * rank, half_tokens)
    part = lax.all_to_all(part, "tensor", 0, 0)
    proj = jnp.sum(part.astype(jnp.float32), axis=0)
    position = (k & 1) * half_tokens + jnp.arange(half_tokens, dtype=jnp.int32)
    kept = position < lengths[(k >> 1) & 3]
    grad = jnp.where(kept[None, :], proj[rank:], 0.0)
    outer = jnp.einsum("as,bs->ab", grad, proj[:rank], precision=HIGH)
    outer = outer.reshape(2, 1, rank // 4, 2 * rank)
    outer = jnp.broadcast_to(outer, (2, 4, rank // 4, 2 * rank)).reshape(8, rank // 4, 2 * rank)
    groups = [list(range(8)), list(range(8, 16))]
    outer = lax.all_to_all(outer, "tensor", 0, 0, axis_index_groups=groups)
    features = outer.reshape(examples, 2, half_feats).sum(axis=1)

    scores = split_dot(features, test_block)
    scores = lax.all_to_all(jnp.broadcast_to(scores[None], (GROUP, examples, block)), "tensor", 0, 0)
    scores = scores.reshape(2, 2, 4, examples, block).sum(axis=(0, 1))
    return jnp.concatenate([scores[0], scores[2], scores[3], scores[1]], axis=1)


def solution(mesh):
    return jax.shard_map(
        shards,
        mesh=mesh,
        in_specs=(
            P(None, "dp", None, "tensor"),
            P(None, "dp", None, "tensor"),
            P(None, "tensor", None),
            P(None, "tensor", None),
            P("dp"),
            P(None, "dp", None),
            P("dp"),
        ),
        out_specs=P("dp", None),
        check_vma=False,
    )
```

```python
import jax
import jax.numpy as jnp
from jax import lax
from jax.sharding import PartitionSpec as P

GROUP = 16
HIGH = lax.Precision.HIGHEST
BOTH = ("dp", "tensor")


def index_of(plane, side, layer, y, core, planes):
    return ((plane % planes) * 2 + side) * GROUP + layer * 8 + y * 2 + core


def block_pairs(planes):
    pairs = []
    for plane in range(planes):
        for side in range(2):
            for layer in range(2):
                for y in range(4):
                    for core in range(2):
                        near = side == y // 2
                        if core == 1 and near:
                            continue
                        back, source_side, source_core = (1, 0, 1) if core else (1, 1, 0) if near else (2, 1, 1)
                        source_layer = layer ^ (side != source_side)
                        source = index_of(plane - back, source_side, source_layer, y, source_core, planes)
                        pairs.append((source, index_of(plane, side, layer, y, core, planes)))
    return pairs


def sent_side(side, y, core):
    near = (y >> 1) ^ core
    return jnp.where(side == 1, near, 1 - (y >> 1))


def split_dot(rows, block):
    high = rows.astype(jnp.bfloat16)
    low = (rows - high.astype(jnp.float32)).astype(jnp.bfloat16)
    both = jnp.concatenate([high, low], axis=0)
    out = jnp.einsum("ef,tf->et", both, block, preferred_element_type=jnp.float32)
    return out[: rows.shape[0]] + out[rows.shape[0] :]


def project(values, matrix):
    layers, examples, tokens, width = values.shape
    halves = values.reshape(layers, examples, 2, tokens // 2, width)
    part = jnp.einsum("lehsd,ldr->lehrs", halves, matrix, preferred_element_type=jnp.float32)
    return part.astype(jnp.bfloat16)


def shards(activations, out_grads, proj_in, proj_out, lengths, test_feats, test_slot):
    _, examples, tokens, _ = activations.shape
    rank = proj_in.shape[2]
    block, feats = test_feats.shape[1], test_feats.shape[2]
    half_feats, quarter, half_tokens = feats // 2, feats // 4, tokens // 2
    planes = lax.axis_size("dp") // 2
    k = lax.axis_index("tensor")
    side = lax.axis_index("dp") & 1
    layer, y, core = k >> 3, (k >> 1) & 3, k & 1
    near = side == (y >> 1)

    place = (jnp.arange(block, dtype=jnp.int32)[:, None] == test_slot[None, :]).astype(jnp.bfloat16)

    def ordered(layer, first, width):
        piece = lax.dynamic_slice(test_feats, (layer, 0, first), (1, block, width))[0]
        return jnp.dot(place, piece, preferred_element_type=jnp.float32).astype(jnp.bfloat16)

    moved = ordered(layer ^ side ^ sent_side(side, y, core), y * quarter, quarter)
    moved = lax.ppermute(moved, BOTH, block_pairs(planes))

    sides = [project(activations, proj_in), project(out_grads, proj_out)]
    part = jnp.concatenate(sides, axis=3).reshape(GROUP, 2 * rank, half_tokens)
    part = lax.all_to_all(part, "tensor", 0, 0)
    own = lax.optimization_barrier(ordered(layer, (y & 1) * half_feats, half_feats))
    proj = jnp.sum(part.astype(jnp.float32), axis=0)
    position = core * half_tokens + jnp.arange(half_tokens, dtype=jnp.int32)
    grad = jnp.where((position < lengths[y])[None, :], proj[rank:], 0.0)
    outer = jnp.einsum("as,bs->ab", grad, proj[:rank], precision=HIGH)
    outer = outer.reshape(2, rank // 4, 2 * rank)
    halves = []
    for to_side in range(2):
        for to_y in range(4):
            for to_core in range(2):
                is_own = to_core == 1 and to_side == to_y // 2
                halves.append(outer[to_y % 2 if is_own else to_y // 2])
    groups = [
        [index_of(plane, s, l, t, c, planes) for s in range(2) for t in range(4) for c in range(2)]
        for plane in range(planes)
        for l in range(2)
    ]
    outer = lax.all_to_all(jnp.stack(halves), BOTH, 0, 0, axis_index_groups=groups)
    features = outer.reshape(2 * examples, 2, half_feats).sum(axis=1)
    some = jnp.where((y & 1) == 1, features[:, quarter:], features[:, :quarter])

    from_own = split_dot(features, own)
    scores = jnp.where((core == 1) & near, from_own, split_dot(some, moved))
    scores = jnp.broadcast_to(scores.reshape(2, 1, examples, block), (2, GROUP, examples, block))
    groups = [
        [(plane * 2) * GROUP + place for place in range(2 * GROUP)] for plane in range(planes)
    ]
    scores = lax.all_to_all(
        scores.reshape(2 * GROUP, examples, block), BOTH, 0, 0, axis_index_groups=groups
    )
    got = scores.reshape(2, 2, 4, 2, examples, block).sum(axis=1)
    own_0 = got[0, 0, 1] + got[0, 1, 1]
    own_1 = got[1, 2, 1] + got[1, 3, 1]
    back_1 = got[0, 0, 0] + got[0, 1, 0] + got[1, 2, 0] + got[1, 3, 0]
    back_2 = got[0, 2, 1] + got[0, 3, 1] + got[1, 0, 1] + got[1, 1, 1]
    back_3 = got[0, 2, 0] + got[0, 3, 0] + got[1, 0, 0] + got[1, 1, 0]
    first = jnp.concatenate([own_0, back_1, back_2, back_3], axis=1)
    second = jnp.concatenate([own_1, own_0, back_1, back_2], axis=1)
    return jnp.where(side == 0, first, second)


def solution(mesh):
    return jax.shard_map(
        shards,
        mesh=mesh,
        in_specs=(
            P(None, "dp", None, "tensor"),
            P(None, "dp", None, "tensor"),
            P(None, "tensor", None),
            P(None, "tensor", None),
            P("dp"),
            P(None, "dp", None),
            P("dp"),
        ),
        out_specs=P("dp", None),
        check_vma=False,
    )
```

```python
import jax
import jax.numpy as jnp
from jax import lax
from jax.sharding import PartitionSpec as P

GROUP = 16
HIGH = lax.Precision.HIGHEST


def role(k):
    y0, core = (k >> 1) & 1, k & 1
    tile = y0 + core * (3 - 2 * y0)
    return tile, (k >> 2) & 1


def block_pairs(dp_size):
    pairs = []
    for shard in range(dp_size):
        for k in range(GROUP):
            tile, _ = role(k)
            source = k ^ (8 * (tile & 1))
            pairs.append((((shard - tile) % dp_size) * GROUP + source, shard * GROUP + k))
    return pairs


def split_dot(rows, block):
    high = rows.astype(jnp.bfloat16)
    low = (rows - high.astype(jnp.float32)).astype(jnp.bfloat16)
    both = jnp.concatenate([high, low], axis=0)
    out = jnp.einsum("ef,tf->et", both, block, preferred_element_type=jnp.float32)
    return out[: rows.shape[0]] + out[rows.shape[0] :]


def project(values, matrix, kept=None):
    layers, examples, tokens, width = values.shape
    halves = values.reshape(layers, examples, 2, tokens // 2, width)
    part = jnp.einsum("lehsd,ldr->lehrs", halves, matrix, preferred_element_type=jnp.float32)
    if kept is not None:
        part = jnp.where(kept.reshape(1, examples, 2, 1, tokens // 2), part, 0.0)
    return part.astype(jnp.bfloat16)


def shards(activations, out_grads, proj_in, proj_out, lengths, test_feats, test_slot):
    _, examples, tokens, _ = activations.shape
    rank = proj_in.shape[2]
    block, feats = test_feats.shape[1], test_feats.shape[2]
    half_feats, half_tokens = feats // 2, tokens // 2
    k = lax.axis_index("tensor")

    tile, half = role(k)
    layer = (k >> 3) ^ (tile & 1)
    piece = lax.dynamic_slice(test_feats, (layer, 0, half * half_feats), (1, block, half_feats))[0]
    place = (jnp.arange(block, dtype=jnp.int32)[:, None] == test_slot[None, :]).astype(jnp.bfloat16)
    ordered = jnp.dot(place, piece, preferred_element_type=jnp.float32).astype(jnp.bfloat16)
    test_block = lax.ppermute(ordered, ("dp", "tensor"), block_pairs(lax.axis_size("dp")))

    kept = jnp.arange(tokens, dtype=jnp.int32)[None, :] < lengths[:, None]
    sides = [project(activations, proj_in), project(out_grads, proj_out, kept)]
    part = jnp.concatenate(sides, axis=3).reshape(GROUP, 2 * rank, half_tokens)
    part = lax.all_to_all(part, "tensor", 0, 0)
    proj = jnp.sum(part.astype(jnp.float32), axis=0)
    outer = jnp.einsum("as,bs->ab", proj[rank:], proj[:rank], precision=HIGH)
    outer = outer.reshape(2, 1, rank // 4, 2 * rank)
    outer = jnp.broadcast_to(outer, (2, 4, rank // 4, 2 * rank)).reshape(8, rank // 4, 2 * rank)
    groups = [list(range(8)), list(range(8, 16))]
    outer = lax.all_to_all(outer, "tensor", 0, 0, axis_index_groups=groups)
    features = outer.reshape(examples, 2, half_feats).sum(axis=1)

    scores = split_dot(features, test_block)
    scores = lax.all_to_all(jnp.broadcast_to(scores[None], (GROUP, examples, block)), "tensor", 0, 0)
    scores = scores.reshape(2, 2, 4, examples, block).sum(axis=(0, 1))
    return jnp.concatenate([scores[0], scores[2], scores[3], scores[1]], axis=1)


def solution(mesh):
    return jax.shard_map(
        shards,
        mesh=mesh,
        in_specs=(
            P(None, "dp", None, "tensor"),
            P(None, "dp", None, "tensor"),
            P(None, "tensor", None),
            P(None, "tensor", None),
            P("dp"),
            P(None, "dp", None),
            P("dp"),
        ),
        out_specs=P("dp", None),
        check_vma=False,
    )
```

```python
import jax
import jax.numpy as jnp
from jax import lax
from jax.sharding import PartitionSpec as P

GROUP = 16
HIGH = lax.Precision.HIGHEST
BOTH = ("dp", "tensor")


def block_pairs(shard_count, tiles):
    return [
        (shard * GROUP + k, ((shard + tiles[k & 1]) % shard_count) * GROUP + k)
        for shard in range(shard_count)
        for k in range(GROUP)
    ]


def split_dot(rows, block):
    high = rows.astype(jnp.bfloat16)
    low = (rows - high.astype(jnp.float32)).astype(jnp.bfloat16)
    both = jnp.concatenate([high, low], axis=0)
    out = jnp.einsum("ef,tf->et", both, block, preferred_element_type=jnp.float32)
    return out[: rows.shape[0]] + out[rows.shape[0] :]


def project(values, matrix, kept=None):
    layers, examples, tokens, width = values.shape
    halves = values.reshape(layers, examples, 2, tokens // 2, width)
    part = jnp.einsum("lehsd,ldr->lehrs", halves, matrix, preferred_element_type=jnp.float32)
    if kept is not None:
        part = jnp.where(kept.reshape(1, examples, 2, 1, tokens // 2), part, 0.0)
    return part.astype(jnp.bfloat16)


def shards(activations, out_grads, proj_in, proj_out, lengths, test_feats, test_slot):
    _, examples, tokens, _ = activations.shape
    rank = proj_in.shape[2]
    block, quarter = test_feats.shape[1], test_feats.shape[2] // 4
    half_tokens = tokens // 2
    shard_count = lax.axis_size("dp")
    k = lax.axis_index("tensor")

    start = (k >> 3, 0, ((k >> 1) & 3) * quarter)
    piece = lax.dynamic_slice(test_feats, start, (1, block, quarter))[0]
    place = (jnp.arange(block, dtype=jnp.int32)[:, None] == test_slot[None, :]).astype(jnp.bfloat16)
    ordered = jnp.dot(place, piece, preferred_element_type=jnp.float32).astype(jnp.bfloat16)
    odd_block = lax.ppermute(ordered, BOTH, block_pairs(shard_count, (1, 3)))
    even_block = lax.ppermute(ordered, BOTH, block_pairs(shard_count, (2, 0)))

    kept = jnp.arange(tokens, dtype=jnp.int32)[None, :] < lengths[:, None]
    sides = [project(activations, proj_in), project(out_grads, proj_out, kept)]
    part = jnp.concatenate(sides, axis=3).reshape(GROUP, 2 * rank, half_tokens)
    part = lax.all_to_all(part, "tensor", 0, 0)
    proj = jnp.sum(part.astype(jnp.float32), axis=0)
    outer = jnp.einsum("as,bs->ab", proj[rank:], proj[:rank], precision=HIGH)
    outer = outer.reshape(4, 1, rank // 8, 2 * rank)
    outer = jnp.broadcast_to(outer, (4, 2, rank // 8, 2 * rank)).reshape(8, rank // 8, 2 * rank)
    groups = [list(range(8)), list(range(8, 16))]
    outer = lax.all_to_all(outer, "tensor", 0, 0, axis_index_groups=groups)
    features = outer.reshape(examples, 2, quarter).sum(axis=1)

    scores = jnp.concatenate([split_dot(features, odd_block), split_dot(features, even_block)], axis=0)
    scores = jnp.broadcast_to(scores[None], (GROUP, 2 * examples, block))
    scores = lax.all_to_all(scores, "tensor", 0, 0)
    scores = scores.reshape(GROUP // 2, 2, 2, examples, block).sum(axis=0)
    return jnp.concatenate([scores[1, 1], scores[0, 0], scores[0, 1], scores[1, 0]], axis=1)


def solution(mesh):
    return jax.shard_map(
        shards,
        mesh=mesh,
        in_specs=(
            P(None, "dp", None, "tensor"),
            P(None, "dp", None, "tensor"),
            P(None, "tensor", None),
            P(None, "tensor", None),
            P("dp"),
            P(None, "dp", None),
            P("dp"),
        ),
        out_specs=P("dp", None),
        check_vma=False,
    )
```

```python
import jax
import jax.numpy as jnp
from jax import lax
from jax.sharding import PartitionSpec as P

GROUP = 16
HIGH = lax.Precision.HIGHEST
BOTH = ("dp", "tensor")


def block_pairs(shard_count, tiles):
    return [
        (shard * GROUP + k, ((shard + tiles[k & 1]) % shard_count) * GROUP + (k ^ (8 * (tiles[k & 1] & 1))))
        for shard in range(shard_count)
        for k in range(GROUP)
    ]


def split_dot(rows, block):
    high = rows.astype(jnp.bfloat16)
    low = (rows - high.astype(jnp.float32)).astype(jnp.bfloat16)
    both = jnp.concatenate([high, low], axis=0)
    out = jnp.einsum("ef,tf->et", both, block, preferred_element_type=jnp.float32)
    return out[: rows.shape[0]] + out[rows.shape[0] :]


def project(values, matrix, kept=None):
    layers, examples, tokens, width = values.shape
    halves = values.reshape(layers, examples, 2, tokens // 2, width)
    part = jnp.einsum("lehsd,ldr->lehrs", halves, matrix, preferred_element_type=jnp.float32)
    if kept is not None:
        part = jnp.where(kept.reshape(1, examples, 2, 1, tokens // 2), part, 0.0)
    return part.astype(jnp.bfloat16)


def shards(activations, out_grads, proj_in, proj_out, lengths, test_feats, test_slot):
    _, examples, tokens, _ = activations.shape
    rank = proj_in.shape[2]
    block, quarter = test_feats.shape[1], test_feats.shape[2] // 4
    half_tokens = tokens // 2
    shard_count = lax.axis_size("dp")
    k = lax.axis_index("tensor")

    start = (k >> 3, 0, ((k >> 1) & 3) * quarter)
    piece = lax.dynamic_slice(test_feats, start, (1, block, quarter))[0]
    place = (jnp.arange(block, dtype=jnp.int32)[:, None] == test_slot[None, :]).astype(jnp.bfloat16)
    ordered = jnp.dot(place, piece, preferred_element_type=jnp.float32).astype(jnp.bfloat16)
    layer_one = jnp.broadcast_to((k >> 3).astype(jnp.float32), (examples, block))
    ordered, layer_one = lax.optimization_barrier((ordered, layer_one))
    odd_block = lax.ppermute(ordered, BOTH, block_pairs(shard_count, (1, 3)))
    even_block = lax.ppermute(ordered, BOTH, block_pairs(shard_count, (2, 0)))

    kept = jnp.arange(tokens, dtype=jnp.int32)[None, :] < lengths[:, None]
    sides = [project(activations, proj_in), project(out_grads, proj_out, kept)]
    part = jnp.concatenate(sides, axis=3).reshape(GROUP, 2 * rank, half_tokens)
    part = lax.all_to_all(part, "tensor", 0, 0)
    proj = jnp.sum(part.astype(jnp.float32), axis=0)
    outer = jnp.einsum("as,bs->ab", proj[rank:], proj[:rank], precision=HIGH)
    outer = outer.reshape(1, 4, 1, rank // 8, 2 * rank)
    outer = jnp.broadcast_to(outer, (2, 4, 2, rank // 8, 2 * rank)).reshape(GROUP, rank // 8, 2 * rank)
    outer = lax.all_to_all(outer, "tensor", 0, 0)
    features = outer.reshape(2 * examples, 2, quarter).sum(axis=1)

    odd = split_dot(features, odd_block).reshape(2, examples, block)
    even = split_dot(features, even_block).reshape(2, examples, block)
    swap = layer_one > 0.5
    odd = jnp.where(swap, odd[0], odd[1])
    even = jnp.where(swap, even[1], even[0])
    scores = jnp.concatenate([odd, even], axis=0)
    scores = jnp.broadcast_to(scores[None], (GROUP, 2 * examples, block))
    scores = lax.all_to_all(scores, "tensor", 0, 0)
    scores = scores.reshape(GROUP // 2, 2, 2, examples, block).sum(axis=0)
    return jnp.concatenate([scores[1, 1], scores[0, 0], scores[0, 1], scores[1, 0]], axis=1)


def solution(mesh):
    return jax.shard_map(
        shards,
        mesh=mesh,
        in_specs=(
            P(None, "dp", None, "tensor"),
            P(None, "dp", None, "tensor"),
            P(None, "tensor", None),
            P(None, "tensor", None),
            P("dp"),
            P(None, "dp", None),
            P("dp"),
        ),
        out_specs=P("dp", None),
        check_vma=False,
    )
```

```python
import jax
import jax.numpy as jnp
from jax import lax
from jax.sharding import PartitionSpec as P

GROUP = 16
HIGH = lax.Precision.HIGHEST
BOTH = ("dp", "tensor")


def block_pairs(shard_count, tiles):
    return [
        (shard * GROUP + k, ((shard + tiles[k & 1]) % shard_count) * GROUP + (k ^ (8 * (tiles[k & 1] & 1))))
        for shard in range(shard_count)
        for k in range(GROUP)
    ]


def split_dot(rows, block):
    high = rows.astype(jnp.bfloat16)
    low = (rows - high.astype(jnp.float32)).astype(jnp.bfloat16)
    both = jnp.concatenate([high, low], axis=0)
    out = jnp.einsum("ef,tf->et", both, block, preferred_element_type=jnp.float32)
    return out[: rows.shape[0]] + out[rows.shape[0] :]


def project(values, matrix):
    layers, examples, tokens, width = values.shape
    halves = values.reshape(layers, examples, 2, tokens // 2, width)
    part = jnp.einsum("lehsd,ldr->lehrs", halves, matrix, preferred_element_type=jnp.float32)
    return part.astype(jnp.bfloat16)


def shards(activations, out_grads, proj_in, proj_out, lengths, test_feats, test_slot):
    _, examples, tokens, _ = activations.shape
    rank = proj_in.shape[2]
    block, quarter = test_feats.shape[1], test_feats.shape[2] // 4
    half_tokens = tokens // 2
    shard_count = lax.axis_size("dp")
    k = lax.axis_index("tensor")

    start = (k >> 3, 0, ((k >> 1) & 3) * quarter)
    piece = lax.dynamic_slice(test_feats, start, (1, block, quarter))[0]
    place = (jnp.arange(block, dtype=jnp.int32)[:, None] == test_slot[None, :]).astype(jnp.bfloat16)
    ordered = jnp.dot(place, piece, preferred_element_type=jnp.float32).astype(jnp.bfloat16)
    layer_one = jnp.broadcast_to((k >> 3).astype(jnp.float32), (examples, block))
    ordered, layer_one = lax.optimization_barrier((ordered, layer_one))
    odd_block = lax.ppermute(ordered, BOTH, block_pairs(shard_count, (1, 3)))
    even_block = lax.ppermute(ordered, BOTH, block_pairs(shard_count, (2, 0)))

    sides = [project(activations, proj_in), project(out_grads, proj_out)]
    part = jnp.concatenate(sides, axis=3).reshape(GROUP, 2 * rank, half_tokens)
    part = lax.all_to_all(part, "tensor", 0, 0)
    proj = jnp.sum(part.astype(jnp.float32), axis=0)
    position = (k & 1) * half_tokens + jnp.arange(half_tokens, dtype=jnp.int32)
    kept = position < lengths[(k >> 1) & 3]
    grad = jnp.where(kept[None, :], proj[rank:], 0.0)
    outer = jnp.einsum("as,bs->ab", grad, proj[:rank], precision=HIGH)
    outer = outer.reshape(1, 4, 1, rank // 8, 2 * rank)
    outer = jnp.broadcast_to(outer, (2, 4, 2, rank // 8, 2 * rank)).reshape(GROUP, rank // 8, 2 * rank)
    outer = lax.all_to_all(outer, "tensor", 0, 0)
    features = outer.reshape(2 * examples, 2, quarter).sum(axis=1)

    swap = layer_one > 0.5
    odd = split_dot(features, odd_block).reshape(2, examples, block)
    odd = lax.optimization_barrier(jnp.where(swap, odd[0], odd[1]))
    even = split_dot(features, even_block).reshape(2, examples, block)
    even = jnp.where(swap, even[1], even[0])
    scores = jnp.concatenate([odd, even], axis=0)
    scores = jnp.broadcast_to(scores[None], (GROUP, 2 * examples, block))
    scores = lax.all_to_all(scores, "tensor", 0, 0)
    scores = scores.reshape(GROUP // 2, 2, 2, examples, block).sum(axis=0)
    return jnp.concatenate([scores[1, 1], scores[0, 0], scores[0, 1], scores[1, 0]], axis=1)


def solution(mesh):
    return jax.shard_map(
        shards,
        mesh=mesh,
        in_specs=(
            P(None, "dp", None, "tensor"),
            P(None, "dp", None, "tensor"),
            P(None, "tensor", None),
            P(None, "tensor", None),
            P("dp"),
            P(None, "dp", None),
            P("dp"),
        ),
        out_specs=P("dp", None),
        check_vma=False,
    )
```

```python
import jax
import jax.numpy as jnp
from jax import lax
from jax.sharding import PartitionSpec as P

GROUP = 16
HIGH = lax.Precision.HIGHEST
BOTH = ("dp", "tensor")


def block_pairs(shard_count, tiles):
    return [
        (shard * GROUP + k, ((shard + tiles[k & 1]) % shard_count) * GROUP + (k ^ (8 * (tiles[k & 1] & 1))))
        for shard in range(shard_count)
        for k in range(GROUP)
    ]


def split_dot(rows, block):
    high = rows.astype(jnp.bfloat16)
    low = (rows - high.astype(jnp.float32)).astype(jnp.bfloat16)
    both = jnp.concatenate([high, low], axis=0)
    out = jnp.einsum("ef,tf->et", both, block, preferred_element_type=jnp.float32)
    return out[: rows.shape[0]] + out[rows.shape[0] :]


def project(values, matrix):
    layers, examples, tokens, width = values.shape
    halves = values.reshape(layers, examples, 2, tokens // 2, width)
    part = jnp.einsum("lehsd,ldr->lehrs", halves, matrix, preferred_element_type=jnp.float32)
    return part.astype(jnp.bfloat16)


def shards(activations, out_grads, proj_in, proj_out, lengths, test_feats, test_slot):
    _, examples, tokens, _ = activations.shape
    rank = proj_in.shape[2]
    block, quarter = test_feats.shape[1], test_feats.shape[2] // 4
    half_tokens = tokens // 2
    shard_count = lax.axis_size("dp")
    k = lax.axis_index("tensor")

    start = (k >> 3, 0, ((k >> 1) & 3) * quarter)
    piece = lax.dynamic_slice(test_feats, start, (1, block, quarter))[0]
    place = (jnp.arange(block, dtype=jnp.int32)[:, None] == test_slot[None, :]).astype(jnp.bfloat16)
    ordered = jnp.dot(place, piece, preferred_element_type=jnp.float32).astype(jnp.bfloat16)
    layer_one = jnp.broadcast_to((k >> 3).astype(jnp.float32), (examples, quarter))
    ordered, layer_one = lax.optimization_barrier((ordered, layer_one))
    odd_block = lax.ppermute(ordered, BOTH, block_pairs(shard_count, (1, 3)))
    even_block = lax.ppermute(ordered, BOTH, block_pairs(shard_count, (2, 0)))

    sides = [project(activations, proj_in), project(out_grads, proj_out)]
    part = jnp.concatenate(sides, axis=3).reshape(GROUP, 2 * rank, half_tokens)
    part = lax.all_to_all(part, "tensor", 0, 0)
    proj = jnp.sum(part.astype(jnp.float32), axis=0)
    position = (k & 1) * half_tokens + jnp.arange(half_tokens, dtype=jnp.int32)
    kept = position < lengths[(k >> 1) & 3]
    grad = jnp.where(kept[None, :], proj[rank:], 0.0)
    outer = jnp.einsum("as,bs->ab", grad, proj[:rank], precision=HIGH)
    outer = outer.reshape(1, 4, 1, rank // 8, 2 * rank)
    outer = jnp.broadcast_to(outer, (2, 4, 2, rank // 8, 2 * rank)).reshape(GROUP, rank // 8, 2 * rank)
    outer = lax.all_to_all(outer, "tensor", 0, 0)
    features = outer.reshape(2 * examples, 2, quarter).sum(axis=1)

    swap = layer_one > 0.5
    odd_rows = jnp.where(swap, features[:examples], features[examples:])
    even_rows = jnp.where(swap, features[examples:], features[:examples])
    odd = lax.optimization_barrier(split_dot(odd_rows, odd_block))
    even = split_dot(even_rows, even_block)
    scores = jnp.broadcast_to(jnp.stack([odd, even])[None], (GROUP, 2, examples, block))
    scores = lax.all_to_all(scores, "tensor", 0, 0)
    scores = scores.reshape(GROUP // 2, 2, 2, examples, block).sum(axis=0)
    return jnp.concatenate([scores[1, 1], scores[0, 0], scores[0, 1], scores[1, 0]], axis=1)


def solution(mesh):
    return jax.shard_map(
        shards,
        mesh=mesh,
        in_specs=(
            P(None, "dp", None, "tensor"),
            P(None, "dp", None, "tensor"),
            P(None, "tensor", None),
            P(None, "tensor", None),
            P("dp"),
            P(None, "dp", None),
            P("dp"),
        ),
        out_specs=P("dp", None),
        check_vma=False,
    )
```

```python
import jax
import jax.numpy as jnp
from jax import lax
from jax.sharding import PartitionSpec as P

GROUP = 16
HIGH = lax.Precision.HIGHEST
BOTH = ("dp", "tensor")


def block_pairs(shard_count, tiles):
    return [
        (shard * GROUP + k, ((shard + tiles[k & 1]) % shard_count) * GROUP + (k ^ (8 * (tiles[k & 1] & 1))))
        for shard in range(shard_count)
        for k in range(GROUP)
    ]


def split_dot(rows, block):
    high = rows.astype(jnp.bfloat16)
    low = (rows - high.astype(jnp.float32)).astype(jnp.bfloat16)
    both = jnp.concatenate([high, low], axis=0)
    out = jnp.einsum("ef,tf->et", both, block, preferred_element_type=jnp.float32)
    return out[: rows.shape[0]] + out[rows.shape[0] :]


def project(values, matrix):
    layers, examples, tokens, width = values.shape
    halves = values.reshape(layers, examples, 2, tokens // 2, width)
    part = jnp.einsum("lehsd,ldr->lehrs", halves, matrix, preferred_element_type=jnp.float32)
    return part.astype(jnp.bfloat16)


def shards(activations, out_grads, proj_in, proj_out, lengths, test_feats, test_slot):
    _, examples, tokens, _ = activations.shape
    rank = proj_in.shape[2]
    block, quarter = test_feats.shape[1], test_feats.shape[2] // 4
    half_tokens = tokens // 2
    shard_count = lax.axis_size("dp")
    k = lax.axis_index("tensor")

    start = (k >> 3, 0, ((k >> 1) & 3) * quarter)
    piece = lax.dynamic_slice(test_feats, start, (1, block, quarter))[0]
    place = (jnp.arange(block, dtype=jnp.int32)[:, None] == test_slot[None, :]).astype(jnp.bfloat16)
    ordered = jnp.dot(place, piece, preferred_element_type=jnp.float32).astype(jnp.bfloat16)
    odd_block = lax.ppermute(ordered, BOTH, block_pairs(shard_count, (1, 3)))
    even_block = lax.ppermute(ordered, BOTH, block_pairs(shard_count, (2, 0)))

    sides = [project(activations, proj_in), project(out_grads, proj_out)]
    part = jnp.concatenate(sides, axis=3).reshape(GROUP, 2 * rank, half_tokens)
    part = lax.all_to_all(part, "tensor", 0, 0)
    proj = jnp.sum(part.astype(jnp.float32), axis=0)
    layer_one = jnp.broadcast_to((k >> 3).astype(jnp.float32), (examples, quarter))
    proj, layer_one = lax.optimization_barrier((proj, layer_one))
    position = (k & 1) * half_tokens + jnp.arange(half_tokens, dtype=jnp.int32)
    kept = position < lengths[(k >> 1) & 3]
    grad = jnp.where(kept[None, :], proj[rank:], 0.0)
    outer = jnp.einsum("as,bs->ab", grad, proj[:rank], precision=HIGH)
    outer = outer.reshape(1, 4, 1, rank // 8, 2 * rank)
    outer = jnp.broadcast_to(outer, (2, 4, 2, rank // 8, 2 * rank)).reshape(GROUP, rank // 8, 2 * rank)
    outer = lax.all_to_all(outer, "tensor", 0, 0)
    features = outer.reshape(2 * examples, 2, quarter).sum(axis=1)

    swap = layer_one > 0.5
    odd_rows = jnp.where(swap, features[:examples], features[examples:])
    even_rows = jnp.where(swap, features[examples:], features[:examples])
    odd = lax.optimization_barrier(split_dot(odd_rows, odd_block))
    even = split_dot(even_rows, even_block)
    scores = jnp.concatenate([odd, even], axis=0)
    scores = jnp.broadcast_to(scores[None], (GROUP, 2 * examples, block))
    scores = lax.all_to_all(scores, "tensor", 0, 0)
    scores = scores.reshape(GROUP // 2, 2, 2, examples, block).sum(axis=0)
    return jnp.concatenate([scores[1, 1], scores[0, 0], scores[0, 1], scores[1, 0]], axis=1)


def solution(mesh):
    return jax.shard_map(
        shards,
        mesh=mesh,
        in_specs=(
            P(None, "dp", None, "tensor"),
            P(None, "dp", None, "tensor"),
            P(None, "tensor", None),
            P(None, "tensor", None),
            P("dp"),
            P(None, "dp", None),
            P("dp"),
        ),
        out_specs=P("dp", None),
        check_vma=False,
    )
```
